32 devices in a mesh: role: 2 (over core), dp: 4 (over z), mp: 4 (over y, x).
Axes of the slice: x: 2, y: 2, z: 4, core: 2. Of those that a mesh axis runs over, the one named last changes fastest.
Arguments:
- noise: bfloat16 [512, 3072], P('dp', 'mp'), may hold values from -6 to 6
- gen_gain: float32 [3072], replicated, may hold values from 0.25 to 1.75
- gen_weight: bfloat16 [3072, 3072], P('dp', 'mp'), may hold values from -0.109375 to 0.109375
- routes: int32 [128, 1], replicated, may hold values from 0 to 3; in each aligned block of 32 rows (0 to 31, 32 to 63, ...) at most 16 rows name the same one
- critic_noise: bfloat16 [1024, 3072], P('dp', 'mp'), may hold values from -6 to 6
- critic_steps: int32 [256], P('dp'), may hold values from 20 to 979
- crit_mod: float32 [2, 2, 3072], P('role'), may hold values from -3 to 3
- crit_first: bfloat16 [2, 3072, 3072], P('role', 'dp', 'mp'), may hold values from -0.109375 to 0.109375
- crit_second: bfloat16 [2, 3072, 3072], P('role', 'dp', 'mp'), may hold values from -0.109375 to 0.109375
Outputs:
- noise_grad: float32 [512, 4, 2, 384], P('dp', 'mp', 'role')
- grad_first: float32 [2, 3072, 3072], P('role', 'dp', 'mp')
- grad_second: float32 [2, 3072, 3072], P('role', 'dp', 'mp')
The draws below stay inside these ranges and needn't reach their ends.
Inputs may be any that keep to these rules, and one draw needn't show every extreme that they name: `routes`: within the 32 rows of one index of dp, no value appears more than 16 times, and in every draw some value appears exactly 16 times in some such block.
All inputs are finite; a program needn't handle non-finite values.
Results may differ from the reference program's by a relative error of at most 0.01.
Values may be sent and summed in bfloat16 or wider, within the bound.
No kernel may reach another device: no remote copies, remote signals or barrier semaphores. Data moves between devices by JAX's collectives and lax.ppermute only.
A program may use at most 128 MiB of HBM per device.

```python
import math
import jax
import jax.numpy as jnp
import numpy as np
from jax import lax

D = 3072
TOK_DEV = 128
BT = 4
NB = 32
MOST = 16
TOKENS = 512
BLOCKS = 128
CTOK = 1024
CBLOCKS = 256
HALFW = 384
N_DP = 4
N_MP = 4


def plant(values, stream_key, smallest, largest):
    spot = [jax.random.randint(jax.random.fold_in(stream_key, axis), (), 0, length) for axis, length in enumerate(values.shape)]
    widest = values.shape.index(max(values.shape))
    next_to = spot[:widest] + [(spot[widest] + 1) % values.shape[widest]] + spot[widest + 1:]
    return values.at[tuple(spot)].set(smallest).at[tuple(next_to)].set(largest)


def level_of(rng, extent, split, smallest, largest):
    def one(position, parts):
        steps = jax.random.uniform(jax.random.fold_in(jax.random.fold_in(rng, 6), position), (parts,), jnp.float32, smallest / len(split), largest / len(split))
        return jnp.repeat(jnp.exp(steps), extent[position] // parts).reshape((-1,) + (1,) * (len(extent) - position - 1))

    factor_of = one(*split[0])
    for cut in split[1:]:
        factor_of = factor_of * one(*cut)
    return factor_of


def deal_out(stream_key, own, number, rows, number_of, top, limit, skew):
    order = jax.random.permutation(stream_key, number_of)
    heavy_load, ordinary = shares(number_of, rows * top, limit, skew, True), shares(number_of, rows * top, limit, skew, False)
    places = jnp.arange(number_of)

    def named(tallies, turn):
        used = int((tallies > 0).sum())
        fixed = max(1, used // 4)
        passed = fixed + (places - fixed + turn * (used - fixed)) % max(1, number_of - fixed)
        return jnp.zeros((number_of,), jnp.int32).at[order[jnp.where(places < fixed, places, passed)]].set(jnp.asarray(tallies, jnp.int32))

    tallies = jnp.where(number % 4 == 0, named(heavy_load, number // 4), named(ordinary, number - number // 4 - 1))
    mixed = jax.random.permutation(jax.random.fold_in(own, 3), number_of)
    source_of, sink = mixed[0:number_of // 2 * 2:2], mixed[1:number_of // 2 * 2:2]
    room = jnp.minimum(tallies[source_of] - 1, limit - tallies[sink]) // 2
    room = jnp.where((source_of == order[0]) | (sink == order[0]) | (tallies[sink] == 0), 0, jnp.maximum(room, 0))
    passed = jax.random.randint(jax.random.fold_in(own, 4), (number_of // 2,), 0, 1 << 20) % (room + 1)
    tallies = tallies.at[source_of].add(-passed).at[sink].add(passed)
    items = jnp.searchsorted(jnp.cumsum(tallies), jnp.arange(rows * top), side="right").astype(jnp.int32)
    table = items.reshape(top, rows).T
    table = table[jax.random.permutation(jax.random.fold_in(own, 1), rows)]
    turn = jax.random.randint(jax.random.fold_in(own, 2), (rows, 1), 0, top)
    return jnp.take_along_axis(table, (jnp.arange(top)[None, :] + turn) % top, axis=1)


def shares(number_of, total, limit, lean, full):
    portions = [(1 << 20) // math.isqrt(standing ** lean) + 1 for standing in range(1, number_of + 1)]
    largest = limit if full else min(limit, max(-(-total // number_of), total * portions[0] // sum(portions)))
    least = 1 if total - largest >= number_of - 1 else 0
    holding, spare = [largest] + [least] * (number_of - 1), total - largest - least * (number_of - 1)
    while spare > 0:
        free = [i for i in range(1, number_of) if holding[i] < largest] or [i for i in range(1, number_of) if holding[i] < limit]
        whole, remaining = sum([portions[i] for i in free]), spare
        for i in free:
            extra = min(limit - holding[i], max(1, remaining * portions[i] // whole), spare)
            holding[i] = holding[i] + extra
            spare = spare - extra
    return np.array(holding)


def scatter_about(stream_key, extent, deviation, bound, split=(), held_as=jnp.bfloat16):
    result = jax.random.normal(stream_key, extent, jnp.float32) * deviation
    if len(split) > 0:
        result = level_of(stream_key, extent, split, -0.22, 0.18) * result
    return jnp.clip(result, min=-bound, max=bound).astype(held_as)


def setup_inputs(seed: int = 0) -> dict:
    arg_keys = jax.random.split(jax.random.key(seed), 10)
    noise = scatter_about(arg_keys[0], (TOKENS, D), 1.0, 6.0, ((0, 4), (1, 4)))
    gen_gain = jnp.clip(1.0 + 0.15 * jax.random.normal(arg_keys[1], (D,), jnp.float32), 0.25, 1.75)
    gen_weight = scatter_about(arg_keys[2], (D, D), D ** -0.5, 0.109375, ((0, 4), (1, 4)))
    routes_keys = jax.random.split(jax.random.fold_in(arg_keys[3], 1), BLOCKS // NB)
    routes_turns = jax.random.permutation(jax.random.fold_in(arg_keys[3], 3), BLOCKS // NB)
    routes = jax.vmap(lambda own, number: deal_out(jax.random.fold_in(arg_keys[3], 2), own, number, NB, N_DP, 1, MOST, 2))(routes_keys, routes_turns).reshape((BLOCKS, 1))
    critic_noise = scatter_about(arg_keys[4], (CTOK, D), 1.0, 6.0, ((0, 4), (1, 4)))
    critic_steps = plant(jax.random.randint(arg_keys[5], (CBLOCKS,), 20, 980), jax.random.fold_in(arg_keys[5], 1), 20, 979).astype(jnp.int32)
    crit_mod = scatter_about(arg_keys[6], (2, 2, D), 1.0, 3.0, ((0, 2),), jnp.float32)
    crit_first = scatter_about(arg_keys[7], (2, D, D), D ** -0.5, 0.109375, ((0, 2), (1, 4), (2, 4)))
    crit_second = scatter_about(arg_keys[8], (2, D, D), D ** -0.5, 0.109375, ((0, 2), (1, 4), (2, 4)))
    return {"noise": noise, "gen_gain": gen_gain, "gen_weight": gen_weight, "routes": routes, "critic_noise": critic_noise, "critic_steps": critic_steps, "crit_mod": crit_mod, "crit_first": crit_first, "crit_second": crit_second}


epsilon = 1e-06
levels = 1000.0

def norm_act(field, scale):
    root = lax.rsqrt(lax.optimization_barrier(jnp.mean(field * field, axis=-1, keepdims=True)) + epsilon)
    normed = field * root
    shaped = normed * scale
    return (jax.nn.silu(shaped).astype(jnp.bfloat16), normed, shaped, root)

def slope(shaped):
    sigma = jax.nn.sigmoid(shaped)
    return sigma * (1.0 + shaped * (1.0 - sigma))

def norm_back(grad_act, normed, shaped, root, scale):
    grad_norm = grad_act * slope(shaped) * scale
    return root * (grad_norm - normed * lax.optimization_barrier(jnp.mean(grad_norm * normed, axis=-1, keepdims=True)))

def rounded(value):
    return lax.optimization_barrier(value.astype(jnp.bfloat16)).astype(jnp.float32)

def column_sum(left, weight):
    width = D // N_MP
    total = jnp.zeros((left.shape[0], D), jnp.float32)
    for block in range(N_MP):
        piece = jnp.dot(left[:, block * width:(block + 1) * width], weight[:, block * width:(block + 1) * width].T, preferred_element_type=jnp.float32)
        total = total + rounded(piece)
    return total

def group_sum(left, right):
    count = left.shape[0] // N_DP

    def step(total, group):
        start = (group * count).astype(jnp.int32)
        part_left = lax.dynamic_slice_in_dim(left, start, count, 0)
        part_right = lax.dynamic_slice_in_dim(right, start, count, 0)
        term = lax.dot_general(part_left, part_right, (((0,), (0,)), ((), ())), preferred_element_type=jnp.float32)
        return (total + rounded(term), None)
    total, _ = lax.scan(step, jnp.zeros((D, D), jnp.float32), jnp.arange(N_DP, dtype=jnp.int32))
    return total

def reference(noise, gen_gain, gen_weight, routes, critic_noise, critic_steps, crit_mod, crit_first, crit_second):
    gen_act, gen_normed, gen_shaped, gen_root = norm_act(noise.astype(jnp.float32), gen_gain[None, :])
    generated = (noise.astype(jnp.float32) + jnp.dot(gen_act, gen_weight, preferred_element_type=jnp.float32)).astype(jnp.bfloat16)
    target_index = routes[:, 0].astype(jnp.int32)
    index = jnp.arange(BLOCKS, dtype=jnp.int32)
    source = index // NB
    earlier = (target_index[:, None] == target_index[None, :]) & (source[:, None] == source[None, :]) & (index[None, :] < index[:, None])
    rank = lax.optimization_barrier(jnp.sum(earlier.astype(jnp.int32), axis=1)).astype(jnp.int32)
    slot = (target_index * (N_DP * MOST) + source * MOST + rank).astype(jnp.int32)
    clean = jnp.zeros((CBLOCKS, BT, D), jnp.bfloat16).at[slot].set(generated.reshape(BLOCKS, BT, D)).reshape(CTOK, D)
    valid = jnp.repeat(jnp.zeros((CBLOCKS,), jnp.float32).at[slot].set(1.0), BT)[:, None]
    level = jnp.repeat(critic_steps.astype(jnp.float32) / levels, BT)[:, None]
    clean_f = clean.astype(jnp.float32)
    noise_f = critic_noise.astype(jnp.float32)
    noisy = ((1.0 - level) * clean_f + level * noise_f).astype(jnp.bfloat16)
    target = noise_f - clean_f
    preds = []
    firsts = []
    seconds = []
    for network in range(2):
        scale_one = 1.0 + level * crit_mod[network, 0][None, :]
        scale_two = 1.0 + level * crit_mod[network, 1][None, :]
        first, _, _, _ = norm_act(noisy.astype(jnp.float32), scale_one)
        hidden = (noisy.astype(jnp.float32) + jnp.dot(first, crit_first[network], preferred_element_type=jnp.float32)).astype(jnp.bfloat16)
        second, normed, shaped, root = norm_act(hidden.astype(jnp.float32), scale_two)
        pred = (hidden.astype(jnp.float32) + jnp.dot(second, crit_second[network], preferred_element_type=jnp.float32)).astype(jnp.bfloat16)
        delta = ((pred.astype(jnp.float32) - target) * valid / TOK_DEV).astype(jnp.bfloat16)
        seconds.append(group_sum(second, delta))
        carried = column_sum(delta, crit_second[network])
        upstream = (delta.astype(jnp.float32) + norm_back(carried, normed, shaped, root, scale_two)).astype(jnp.bfloat16)
        firsts.append(group_sum(first, upstream))
        preds.append(pred)
    gap = (1.0 - level) * (preds[1].astype(jnp.float32) - preds[0].astype(jnp.float32))
    back_blocks = gap.astype(jnp.bfloat16).reshape(CBLOCKS, BT, D)[slot]
    returned = back_blocks.reshape(TOKENS, D)
    carried_gen = column_sum(returned, gen_weight)
    noise_grad = returned.astype(jnp.float32) + norm_back(carried_gen, gen_normed, gen_shaped, gen_root, gen_gain[None, :])
    return (noise_grad.reshape(TOKENS, N_MP, 2, HALFW), jnp.stack(firsts), jnp.stack(seconds))
```

```python
import jax
import jax.numpy as jnp
from jax import lax
from jax.sharding import PartitionSpec as P

TOK_DEV = 128
BT = 4

epsilon = 1e-06
levels = 1000.0

bf16 = jnp.bfloat16
f32 = jnp.float32


def crossed():
    count = lax.axis_size("dp")
    return count == lax.axis_size("mp") and count in (2, 4)


def swap(block, axis, apart):
    count = lax.axis_size(axis)
    return lax.ppermute(block, axis, [(i, i ^ apart) for i in range(count)])


def with_others(block, axis):
    return [block] + [swap(block, axis, k) for k in range(1, lax.axis_size(axis))]


def exchange(blocks, axis):
    return [blocks[0]] + [swap(blocks[k], axis, k) for k in range(1, len(blocks))]


def arrange(blocks, shift):
    bit = 1
    while bit < len(blocks):
        flip = (shift & bit) != 0
        blocks = [jnp.where(flip, blocks[k ^ bit], blocks[k]) for k in range(len(blocks))]
        bit *= 2
    return blocks


def diagonal():
    return lax.axis_index("dp") ^ lax.axis_index("mp")


def group_order(per_group):
    if crossed():
        return jnp.stack(arrange(list(per_group), lax.axis_index("dp")))
    return per_group


def spread(block):
    if crossed():
        return jnp.stack(with_others(block, "dp"))
    return lax.all_gather(block, "dp", axis=0)


def to_groups(blocks):
    if crossed():
        return jnp.stack(exchange(arrange(list(blocks), lax.axis_index("dp")), "dp"))
    return lax.all_to_all(blocks, "dp", split_axis=0, concat_axis=0, tiled=True)


def turn(block):
    width = block.shape[1] * lax.axis_size("mp")
    if crossed():
        pieces = with_others(block, "mp")
        square = sum(jnp.sum(jnp.square(p.astype(f32)), axis=-1) for p in pieces)
        rows = jnp.stack(exchange(arrange(pieces, diagonal()), "dp"))
    else:
        wide = lax.all_gather(block, "mp", axis=1, tiled=True)
        square = jnp.sum(jnp.square(wide.astype(f32)), axis=-1)
        rows = lax.all_to_all(wide, "dp", split_axis=1, concat_axis=0, tiled=True)
        rows = rows.reshape(-1, block.shape[0], rows.shape[1])
    return rows, spread(lax.rsqrt(square / width + epsilon))


def sum_groups(terms):
    sent = terms.astype(bf16)
    if crossed():
        total = terms[0]
        for k in range(1, terms.shape[0]):
            total = total + swap(sent[k], "dp", k).astype(f32)
        return total
    flat = sent.reshape(-1, terms.shape[2])
    return lax.psum_scatter(flat, "dp", scatter_dimension=0, tiled=True).astype(f32)


def chunk(rows):
    if crossed():
        return lax.dynamic_index_in_dim(rows, diagonal(), 0, keepdims=False)
    shares = rows.reshape((lax.axis_size("mp"), -1) + rows.shape[2:])
    return lax.dynamic_index_in_dim(shares, lax.axis_index("mp"), 0, keepdims=False)


def sum_columns(terms):
    if crossed():
        own = chunk(terms)
        sent = arrange(list(terms.astype(bf16)), diagonal())
        for m in range(1, len(sent)):
            own = own + swap(sent[m], "mp", m).astype(f32)
        return own
    flat = terms.astype(bf16).reshape(-1, terms.shape[2])
    return lax.psum_scatter(flat, "mp", scatter_dimension=0, tiled=True).astype(f32)


def to_columns(share, groups):
    if crossed():
        shift = diagonal()
        blocks = exchange(arrange(with_others(share, "dp"), shift), "mp")
        return jnp.stack(arrange(blocks, shift))
    wide = lax.all_gather(share, "dp", axis=1, tiled=True)
    cols = lax.all_to_all(wide, "mp", split_axis=1, concat_axis=0, tiled=True)
    return cols.reshape(groups, -1, cols.shape[1])


def to_home(share, groups):
    if crossed():
        count = lax.axis_size("dp")
        pairs = [(a * count + b, b * count + a) for a in range(count) for b in range(count)]
        return lax.ppermute(share, ("dp", "mp"), pairs)
    return lax.dynamic_index_in_dim(
        to_columns(share, groups), lax.axis_index("dp"), 0, keepdims=False
    )


def other_role(block):
    return lax.ppermute(block, "role", [(0, 1), (1, 0)])


def norm(rows, roots, scale):
    normed = rows.astype(f32) * roots[..., None]
    return normed, normed * scale


def slope(shaped):
    sigma = jax.nn.sigmoid(shaped)
    return sigma * (1.0 + shaped * (1.0 - sigma))


def times(left, weight):
    return lax.dot_general(left, weight, (((2,), (0,)), ((), ())), preferred_element_type=f32)


def times_back(left, weight):
    return lax.dot_general(left, weight, (((2,), (1,)), ((), ())), preferred_element_type=f32)


def grad_of(left, right):
    return lax.dot_general(left, right, (((0, 1), (0, 1)), ((), ())), preferred_element_type=f32)


def back(terms, rows, roots, scale, depth):
    owned = sum_columns(terms)
    root = chunk(roots)
    mine = chunk(scale) if scale.ndim == 3 else scale
    normed, shaped = norm(chunk(rows), root, mine)
    grad_norm = owned * slope(shaped) * mine
    inner = jnp.sum(spread(jnp.sum(grad_norm * normed, axis=-1)), axis=0)
    return (root[:, None] * (grad_norm - normed * (inner[:, None] / depth))).astype(bf16)


def shards(
    noise, gen_gain, gen_weight, routes, critic_noise, critic_steps, crit_mod, crit_first, crit_second
):
    groups = lax.axis_size("dp")
    me = lax.axis_index("dp")
    role = lax.axis_index("role")
    tokens, width = noise.shape
    half = tokens // 2
    depth = gen_gain.shape[0]
    deep = gen_weight.shape[0]
    blocks_here = tokens // BT
    most = 2 * blocks_here // groups
    first_w, second_w = crit_first[0], crit_second[0]

    def my_rows(vector):
        return lax.dynamic_slice_in_dim(vector, me * deep, deep, 0)

    def own_first(field, axis):
        return jnp.roll(field, -role * (field.shape[axis] // 2), axis=axis)

    noise_half = lax.dynamic_slice_in_dim(noise, role * half, half, 0)
    gen_rows, gen_roots = turn(noise_half)
    gen_scale = my_rows(gen_gain)
    gen_act = jax.nn.silu(norm(gen_rows, gen_roots, gen_scale)[1]).astype(bf16)
    gen_half = (noise_half.astype(f32) + sum_groups(times(gen_act, gen_weight))).astype(bf16)

    table = group_order(routes.reshape(groups, blocks_here))
    order = jnp.arange(blocks_here, dtype=jnp.int32)
    earlier = (table[:, :, None] == table[:, None, :]) & (order[None, :] < order[:, None])[None]
    rank = jnp.sum(earlier.astype(jnp.int32), axis=2)
    group_ids = group_order(jnp.arange(groups, dtype=jnp.int32)[:, None])
    place = group_ids * most + rank
    steps = spread(critic_steps).reshape(-1)
    critic_of = jnp.repeat(group_ids[:, 0], critic_steps.shape[0])
    place_of = jnp.tile(jnp.arange(critic_steps.shape[0], dtype=jnp.int32), groups)
    hit = (table[:, :, None] == critic_of) & (place[:, :, None] == place_of)
    step_of = jnp.sum(jnp.where(hit, steps, 0), axis=2)
    level = jnp.repeat(own_first(step_of, 1).astype(f32) / levels, BT, axis=1)

    arrived = to_groups(critic_noise.reshape(groups, most * BT, width)).reshape(-1, width)
    mine = 0 if crossed() else me
    table_here, rank_here = own_first(table[mine], 0), own_first(rank[mine], 0)
    row_critic = jnp.repeat(group_ids[:, 0], most)
    row_rank = jnp.tile(jnp.arange(most, dtype=jnp.int32), groups)
    chosen = (table_here[:, None] == row_critic) & (rank_here[:, None] == row_rank)
    chosen = jnp.repeat(jnp.repeat(chosen, BT, axis=0), BT, axis=1)
    within = jnp.arange(tokens)[:, None] % BT == jnp.arange(arrived.shape[0])[None, :] % BT
    crit_noise = jnp.dot((chosen & within).astype(bf16), arrived, preferred_element_type=f32)

    level_here = level[mine][:, None]

    def mix(clean, part):
        return (
            (1.0 - level_here[part]) * clean.astype(f32) + level_here[part] * crit_noise[part]
        ).astype(bf16)

    noisy_half = mix(gen_half, slice(0, half))
    clean = jnp.concatenate([gen_half, other_role(gen_half)])
    noisy = jnp.concatenate([noisy_half, mix(clean[half:], slice(half, None))])

    rows_half, roots_half = turn(noisy_half)
    rows_one = jnp.concatenate([rows_half, other_role(rows_half)], axis=1)
    roots_one = jnp.concatenate([roots_half, other_role(roots_half)], axis=1)
    scale_one = 1.0 + level[:, :, None] * my_rows(crit_mod[0, 0])
    scale_two = 1.0 + level[:, :, None] * my_rows(crit_mod[0, 1])
    first = jax.nn.silu(norm(rows_one, roots_one, scale_one)[1]).astype(bf16)
    hidden = (noisy.astype(f32) + sum_groups(times(first, first_w))).astype(bf16)
    rows_two, roots_two = turn(hidden)
    second = jax.nn.silu(norm(rows_two, roots_two, scale_two)[1]).astype(bf16)
    pred = (hidden.astype(f32) + sum_groups(times(second, second_w))).astype(bf16)
    delta = ((pred.astype(f32) - (crit_noise - clean.astype(f32))) / TOK_DEV).astype(bf16)

    deltas = spread(delta)
    grad_two = grad_of(second, deltas)
    passed = back(times_back(deltas, second_w), rows_two, roots_two, scale_two, depth)
    upstream = (deltas.astype(f32) + to_columns(passed, groups).astype(f32)).astype(bf16)
    grad_one = grad_of(first, upstream)

    mine_pred = pred[:half].astype(f32)
    other_pred = other_role(pred[half:]).astype(f32)
    difference = jnp.where(role == 1, mine_pred - other_pred, other_pred - mine_pred)
    returned = ((1.0 - level_here[:half]) * difference).astype(bf16)
    passed_gen = back(
        times_back(spread(returned), gen_weight), gen_rows, gen_roots, gen_scale, depth
    )
    grad_half = returned.astype(f32) + to_home(passed_gen, groups).astype(f32)
    part = width // 2
    kept = lax.dynamic_slice_in_dim(grad_half, role * part, part, 1)
    got = other_role(lax.dynamic_slice_in_dim(grad_half, (1 - role) * part, part, 1))
    noise_grad = jnp.where(
        role == 0, jnp.concatenate([kept, got]), jnp.concatenate([got, kept])
    )
    return (noise_grad.reshape(tokens, 1, 1, part), grad_one[None], grad_two[None])


def solution(mesh):
    in_specs = (
        P("dp", "mp"),
        P(),
        P("dp", "mp"),
        P(),
        P("dp", "mp"),
        P("dp"),
        P("role", None, None),
        P("role", "dp", "mp"),
        P("role", "dp", "mp"),
    )
    out_specs = (P("dp", "mp", "role", None), P("role", "dp", "mp"), P("role", "dp", "mp"))
    return jax.shard_map(shards, mesh=mesh, in_specs=in_specs, out_specs=out_specs, check_vma=False)
```

```python
import jax
import jax.numpy as jnp
from jax import lax
from jax.sharding import PartitionSpec as P

TOK_DEV = 128
BT = 4

epsilon = 1e-06
levels = 1000.0

bf16 = jnp.bfloat16
f32 = jnp.float32


def crossed():
    count = lax.axis_size("dp")
    return count == lax.axis_size("mp") and count in (2, 4)


def after(value, *events):
    return lax.optimization_barrier((value,) + events)[0]


def after_all(values, *events):
    return list(lax.optimization_barrier(tuple(values) + events)[: len(values)])


def swap(block, axis, apart):
    count = lax.axis_size(axis)
    return lax.ppermute(block, axis, [(i, i ^ apart) for i in range(count)])


def with_others(block, axis):
    return [block] + [swap(block, axis, k) for k in range(1, lax.axis_size(axis))]


def exchange(blocks, axis):
    return [blocks[0]] + [swap(blocks[k], axis, k) for k in range(1, len(blocks))]


def arrange(blocks, shift):
    bit = 1
    while bit < len(blocks):
        flip = (shift & bit) != 0
        blocks = [jnp.where(flip, blocks[k ^ bit], blocks[k]) for k in range(len(blocks))]
        bit *= 2
    return blocks


def diagonal():
    return lax.axis_index("dp") ^ lax.axis_index("mp")


def group_order(per_group):
    if crossed():
        return jnp.stack(arrange(list(per_group), lax.axis_index("dp")))
    return per_group


def spread(block):
    if crossed():
        return jnp.stack(with_others(block, "dp"))
    return lax.all_gather(block, "dp", axis=0)


def to_groups(blocks):
    if crossed():
        return jnp.stack(exchange(arrange(list(blocks), lax.axis_index("dp")), "dp"))
    return lax.all_to_all(blocks, "dp", split_axis=0, concat_axis=0, tiled=True)


def turn(block):
    width = block.shape[1] * lax.axis_size("mp")
    if crossed():
        pieces = with_others(block, "mp")
        square = sum(jnp.sum(jnp.square(p.astype(f32)), axis=-1) for p in pieces)
        root = lax.rsqrt(square / width + epsilon)[:, None]
        high = lax.reduce_precision(root, 8, 7)
        tail = jnp.pad(jnp.concatenate([high, root - high], axis=1), ((0, 0), (0, 126)))
        sent = [jnp.concatenate([p, tail.astype(bf16)], axis=1) for p in arrange(pieces, diagonal())]
        rows = jnp.stack(exchange(sent, "dp"))
        tail = rows[:, :, -128:].astype(f32)
        return rows[:, :, :-128], tail[:, :, 0] + tail[:, :, 1], pieces
    else:
        pieces = [lax.all_gather(block, "mp", axis=1, tiled=True)]
        wide = pieces[0]
        square = jnp.sum(jnp.square(wide.astype(f32)), axis=-1)
        rows = lax.all_to_all(wide, "dp", split_axis=1, concat_axis=0, tiled=True)
        rows = rows.reshape(-1, block.shape[0], rows.shape[1])
    return rows, spread(lax.rsqrt(square / width + epsilon)), pieces


def sum_groups(terms):
    sent = terms.astype(bf16)
    if crossed():
        total = terms[0]
        for k in range(1, terms.shape[0]):
            total = total + swap(sent[k], "dp", k).astype(f32)
        return total
    flat = sent.reshape(-1, terms.shape[2])
    return lax.psum_scatter(flat, "dp", scatter_dimension=0, tiled=True).astype(f32)


def chunk(rows):
    if crossed():
        return lax.dynamic_index_in_dim(rows, diagonal(), 0, keepdims=False)
    shares = rows.reshape((lax.axis_size("mp"), -1) + rows.shape[2:])
    return lax.dynamic_index_in_dim(shares, lax.axis_index("mp"), 0, keepdims=False)


def mirror(block):
    count = lax.axis_size("dp")
    pairs = [(a * count + b, b * count + a) for a in range(count) for b in range(count)]
    return lax.ppermute(block, ("dp", "mp"), pairs)


def to_share(block):
    return mirror(block) if crossed() else chunk(turn(block)[0])


def to_home(share, tokens):
    if crossed():
        return mirror(share)
    wide = lax.all_gather(share, "dp", axis=1, tiled=True)
    cols = lax.all_to_all(wide, "mp", split_axis=1, concat_axis=0, tiled=True)
    return lax.dynamic_slice_in_dim(cols, lax.axis_index("dp") * tokens, tokens, 0)


def other_role(block):
    return lax.ppermute(block, "role", [(0, 1), (1, 0)])


def by_role(own, axis):
    other, first = other_role(own), lax.axis_index("role") == 0
    return jnp.concatenate([jnp.where(first, own, other), jnp.where(first, other, own)], axis=axis)


def pairs_of_two():
    return crossed() and lax.axis_size("mp") == 4


def all_columns(weight):
    if not pairs_of_two():
        return [lax.all_gather(weight, "mp", axis=1, tiled=True)]
    return [weight, swap(weight, "mp", 1), swap(weight, "mp", 2)]


def last_columns(pieces, *events):
    if not pairs_of_two():
        return pieces
    cut = pieces[0].shape[0] // 2
    ends = after(pieces[2][:cut], *events), after(pieces[1][cut:], *events)
    return pieces + [(swap(ends[0], "mp", 1), swap(ends[1], "mp", 2))]


def dot(left, right):
    return jnp.dot(left, right, preferred_element_type=f32)


def dot_back(left, right):
    return lax.dot_general(left, right, (((1,), (1,)), ((), ())), preferred_element_type=f32)


def forward(left, pieces):
    outs = []
    for piece in pieces:
        if isinstance(piece, tuple):
            cut = piece[0].shape[0]
            outs.append(dot(left[:, :cut], piece[0]) + dot(left[:, cut:], piece[1]))
        else:
            outs.append(dot(left, piece))
    if len(outs) == 1:
        flat = outs[0].astype(bf16)
        return lax.psum_scatter(flat, "dp", scatter_dimension=1, tiled=True).astype(f32)
    outs = arrange(outs, diagonal())
    total = outs[0]
    for k in range(1, len(outs)):
        total = total + swap(outs[k].astype(bf16), "dp", k).astype(f32)
    return total


def all_features(share):
    if not pairs_of_two():
        return [lax.all_gather(share, "dp", axis=1, tiled=True)]
    return arrange(with_others(share, "dp"), diagonal())


def backward(blocks, pieces):
    total = 0.0
    for block, piece in zip(blocks, pieces):
        if isinstance(piece, tuple):
            total = total + jnp.concatenate([dot_back(block, p) for p in piece], axis=1)
        else:
            total = total + dot_back(block, piece)
    return total


def to_columns(blocks):
    if len(blocks) == 1:
        return lax.all_to_all(blocks[0], "mp", split_axis=1, concat_axis=0, tiled=True)
    return jnp.concatenate(exchange(blocks, "mp"))


def all_tokens(share):
    if not pairs_of_two():
        return lax.all_gather(share, "mp", axis=0, tiled=True)
    return jnp.concatenate(with_others(share, "mp"))


def sum_dp(value):
    return jnp.sum(spread(value), axis=0)


def norm(rows, root, scale):
    normed = rows.astype(f32) * root[..., None]
    return normed, normed * scale


def root_of(rows, depth):
    square = sum_dp(jnp.sum(jnp.square(rows.astype(f32)), axis=-1))
    return lax.rsqrt(square / depth + epsilon)


def slope(shaped):
    sigma = jax.nn.sigmoid(shaped)
    return sigma * (1.0 + shaped * (1.0 - sigma))


def grad_of(left, right):
    return lax.dot_general(left, right, (((0,), (0,)), ((), ())), preferred_element_type=f32)


def shards(
    noise, gen_gain, gen_weight, routes, critic_noise, critic_steps, crit_mod, crit_first, crit_second
):
    groups = lax.axis_size("dp")
    me = lax.axis_index("dp")
    column = lax.axis_index("mp")
    role = lax.axis_index("role")
    tokens, width = noise.shape
    half = tokens // 2
    depth = gen_gain.shape[0]
    deep = gen_weight.shape[0]
    blocks_here = tokens // BT
    most = 2 * blocks_here // groups
    near = groups // lax.axis_size("mp")
    first_w, second_w = crit_first[0], crit_second[0]

    def my_rows(vector):
        return lax.dynamic_slice_in_dim(vector, me * deep, deep, 0)

    def my_part(field, axis, of):
        part = field.shape[axis] // 2
        return lax.dynamic_slice_in_dim(field, of * part, part, axis)

    def tokens_by_role(own):
        own = own.reshape((near, half) + own.shape[1:])
        both = by_role(own, 1)
        return both.reshape((near * tokens,) + own.shape[2:])

    noise_half = lax.dynamic_slice_in_dim(noise, role * half, half, 0)
    gen_rows, gen_roots, gen_pieces = turn(noise_half)
    gen_scale = my_rows(gen_gain)
    gen_act = jax.nn.silu(norm(gen_rows, gen_roots, gen_scale)[1]).astype(bf16)
    gen_terms = lax.dot_general(
        gen_act, gen_weight, (((2,), (0,)), ((), ())), preferred_element_type=f32
    )
    gen_half = (noise_half.astype(f32) + sum_groups(gen_terms)).astype(bf16)

    table = routes.reshape(groups, blocks_here)
    mine = lax.dynamic_index_in_dim(table, column if crossed() else me, 0, keepdims=False)
    order = jnp.arange(blocks_here, dtype=jnp.int32)
    earlier = (mine[:, None] == mine[None, :]) & (order[None, :] < order[:, None])
    rank = jnp.sum(earlier.astype(jnp.int32), axis=1)
    group_ids = group_order(jnp.arange(groups, dtype=jnp.int32)[:, None])[:, 0]
    row = jnp.arange(groups * most * BT, dtype=jnp.int32)
    row_critic = jnp.repeat(group_ids, most * BT)
    token_rank = jnp.repeat(rank, BT) * BT + jnp.arange(tokens, dtype=jnp.int32) % BT
    chosen = (jnp.repeat(mine, BT)[:, None] == row_critic) & (
        token_rank[:, None] == row % (most * BT)
    )
    chosen = chosen.astype(bf16)
    steps = jnp.repeat(critic_steps.reshape(groups, most), BT, axis=1)[:, :, None]
    packed = jnp.concatenate([steps // 32, steps % 32], axis=2).astype(bf16)
    packed = jnp.pad(packed, ((0, 0), (0, 0), (0, 126)))
    slots = critic_noise.reshape(groups, most * BT, width)
    if crossed():
        carried = jnp.concatenate([my_part(slots, 2, role), packed], axis=2)
        passing = exchange(arrange(list(carried), column), "mp")
        passing = exchange(arrange(after_all(passing, *gen_pieces), diagonal()), "dp")
        share = dot(chosen, jnp.concatenate(passing)).astype(bf16)
        crit_noise = by_role(share[:, :-128], 1).astype(f32)
        step = share[:, -128:].astype(f32)
    else:
        arrived = to_groups(slots).reshape(-1, width)
        crit_noise = to_share(dot(chosen, arrived).astype(bf16)).astype(f32)
        arrived = to_groups(packed).reshape(-1, packed.shape[2])
        step = lax.all_gather(dot(chosen, arrived).astype(bf16), "dp", axis=0)
        step = chunk(step).astype(f32)
    level = ((step[:, 0] * 32.0 + step[:, 1]) / levels)[:, None]

    first_pieces = all_columns(after(first_w, *gen_pieces))
    gen_half = after(gen_half, *first_pieces)
    first_pieces = last_columns(first_pieces, gen_half)
    second_pieces = all_columns(after(second_w, *jax.tree.leaves(first_pieces)))
    clean = tokens_by_role(to_share(gen_half)).astype(f32)
    noisy = ((1.0 - level) * clean + level * crit_noise).astype(bf16)
    scale_one = 1.0 + level * my_rows(crit_mod[0, 0])
    scale_two = 1.0 + level * my_rows(crit_mod[0, 1])
    first = jax.nn.silu(norm(noisy, root_of(noisy, depth), scale_one)[1]).astype(bf16)
    hidden = (noisy.astype(f32) + forward(first, first_pieces)).astype(bf16)
    hidden = after(hidden, *second_pieces)
    second_pieces = last_columns(second_pieces, hidden)
    root = root_of(hidden, depth)
    normed, shaped = norm(hidden, root, scale_two)
    second = jax.nn.silu(shaped).astype(bf16)
    pred = (hidden.astype(f32) + forward(second, second_pieces)).astype(bf16)
    delta = ((pred.astype(f32) - (crit_noise - clean)) / TOK_DEV).astype(bf16)

    def back(grad_act, normed, shaped, root, scale, add_up):
        grad_norm = grad_act * slope(shaped) * scale
        inner = add_up(jnp.sum(grad_norm * normed, axis=-1))
        return root[:, None] * (grad_norm - normed * (inner[:, None] / depth))

    gen_part = my_part(gen_weight, 1, role) if crossed() else gen_weight
    weight_pieces = all_columns(after(gen_part, *jax.tree.leaves(second_pieces)))

    deltas = all_features(delta)
    weight_pieces = last_columns(weight_pieces, *deltas)
    grad_act = backward(deltas, second_pieces)
    upstream = (delta.astype(f32) + back(grad_act, normed, shaped, root, scale_two, sum_dp)).astype(
        bf16
    )
    grad_one = grad_of(all_tokens(first), to_columns(all_features(upstream)))
    grad_two = grad_of(all_tokens(second), to_columns(deltas))

    mine_pred, other_pred = pred.astype(f32), other_role(pred).astype(f32)
    difference = jnp.where(role == 1, mine_pred - other_pred, other_pred - mine_pred)
    returned = after(((1.0 - level) * difference).astype(bf16), *deltas)
    own_rows, own_roots = chunk(gen_rows), chunk(gen_roots)
    gen_root = tokens_by_role(own_roots)
    if crossed():
        kept = my_part(own_rows, 1, role)
        got = other_role(my_part(own_rows, 1, 1 - role))
        noise_rows = jnp.where(
            role == 0, jnp.concatenate([kept, got]), jnp.concatenate([got, kept])
        )
        blocks = after_all(all_features(my_part(returned, 1, role)), upstream)
        terms = backward(blocks, weight_pieces)
        gen_grad = my_part(terms, 1, role) + other_role(my_part(terms, 1, 1 - role))
        gen_scale, returned = my_part(gen_scale, 0, role), my_part(returned, 1, role)

        def add_up(value):
            return sum_dp(value + other_role(value))

    else:
        noise_rows = tokens_by_role(own_rows)
        gen_grad = backward(all_features(returned), weight_pieces)
        add_up = sum_dp
    gen_normed, gen_shaped = norm(noise_rows, gen_root, gen_scale)
    noise_grad = returned.astype(f32) + back(
        gen_grad, gen_normed, gen_shaped, gen_root, gen_scale, add_up
    )
    noise_grad = to_home(noise_grad.astype(bf16), tokens).astype(f32)
    if not crossed():
        noise_grad = my_part(noise_grad, 1, role)
    return (noise_grad.reshape(tokens, 1, 1, -1), grad_one[None], grad_two[None])


def solution(mesh):
    in_specs = (
        P("dp", "mp"),
        P(),
        P("dp", "mp"),
        P(),
        P("dp", "mp"),
        P("dp"),
        P("role", None, None),
        P("role", "dp", "mp"),
        P("role", "dp", "mp"),
    )
    out_specs = (P("dp", "mp", "role", None), P("role", "dp", "mp"), P("role", "dp", "mp"))
    return jax.shard_map(shards, mesh=mesh, in_specs=in_specs, out_specs=out_specs, check_vma=False)
```
